32 devices in a mesh: clip: 2 (over y), tm: 4 (over z), head: 2 (over x), sub: 2 (over core).
Axes of the slice: x: 2, y: 2, z: 4, core: 2. Of those that a mesh axis runs over, the one named last changes fastest.
Arguments:
- queries: bfloat16 [8, 256, 3072], P(('clip', 'tm'), None, ('head', 'sub')), parts along dimension 0, may hold values from -6 to 6, as said below
- keys: bfloat16 [8, 256, 3072], P(('clip', 'tm'), None, ('head', 'sub')), parts along dimension 0, may hold values from -6 to 6, as said below
- values: bfloat16 [8, 256, 3072], P(('clip', 'tm'), None, ('head', 'sub')), parts along dimension 0, may hold values from -6 to 6
- band_table: int32 [4, 4], replicated, may hold values from 0 to 3, as said below
- windows: int32 [7], replicated, may hold values from 1 to 128, as said below
- out_weight: bfloat16 [3072, 3072], P(('head', 'sub')), may hold values from -0.109375 to 0.109375
Outputs:
- mixed: bfloat16 [8, 256, 3072], P(('clip', 'tm'), ('head', 'sub')), parts along dimension 0
The draws below stay inside these ranges and needn't reach their ends.
There are 2 independent parts, one for each index of `clip`. The reference program is written for one: setup_inputs(seed, part) draws one part's arguments, and reference() takes and returns one part's arrays. A program takes and returns all parts, laid end to end along the dimension named above; an argument that names none is the same for every part. Nothing has to cross between parts.
Inputs may be any that keep to these rules, and one draw needn't show every extreme that they name: `queries`: entries of normal law within the range; some rows may be aligned with some key rows. `keys`: entries of normal law within the range; some rows may be aligned with some query rows. `band_table`: Symmetric; 0 exactly on the diagonal; off the diagonal, for frames at distance d it is floor(log2 d) + 1 or one more, never above 6; the pair of frames 0 and 3 takes the one more (up to 6). windows[0] = 128; for k >= 1, windows[k] lies between max(1, 64 // 2**k) and max(that + 1, 128 // 2**k + 1) - 1.
All inputs are finite; a program needn't handle non-finite values.
Results may differ from the reference program's by a relative error of at most 0.015.
Values may be sent and summed in bfloat16 or wider, within the bound.
A program may use at most 64 MiB of HBM per device.

```python
import jax
import jax.numpy as jnp
from jax import lax

D = 3072
HEADS = 24
HEAD = 128
S = 256
NB = 7
FRAMES = 4


def paired_fields(key):
    shape = (FRAMES, S, HEADS * HEAD)
    query = jnp.clip(jax.random.normal(jax.random.fold_in(key, 11), shape, jnp.float32), -6.0, 6.0)
    keyset = jnp.clip(jax.random.normal(jax.random.fold_in(key, 12), shape, jnp.float32), -6.0, 6.0)
    return (query, keyset)


def draw_queries(key, part):
    return paired_fields(key)[0].astype(jnp.bfloat16)


def draw_keys(key, part):
    return paired_fields(key)[1].astype(jnp.bfloat16)


def draw_band_table(key, part):
    index = jnp.arange(FRAMES, dtype=jnp.int32)
    distance = jnp.abs(index[:, None] - index[None, :])
    base = jnp.zeros((FRAMES, FRAMES), jnp.int32)
    for power in range(16):
        base = base + (distance >= 1 << power).astype(jnp.int32)
    jitter = jax.random.randint(jax.random.fold_in(key, 21), (FRAMES, FRAMES), 0, 2).astype(jnp.int32)
    jitter = jnp.triu(jitter, 1)
    jitter = jitter.at[0, FRAMES - 1].set(1)
    jitter = jitter + jnp.transpose(jitter)
    band = jnp.minimum(base + jitter, NB - 1)
    return jnp.where(distance > 0, band, 0).astype(jnp.int32)


def draw_windows(key, part):
    levels = jnp.left_shift(jnp.ones((NB,), jnp.int32), jnp.arange(NB, dtype=jnp.int32))
    lowest = jnp.maximum(1, S // 4 // levels)
    highest = jnp.maximum(lowest + 1, S // 2 // levels + 1)
    spread = jax.random.randint(jax.random.fold_in(key, 31), (NB,), 0, 1 << 20).astype(jnp.int32)
    reach = lowest + spread % (highest - lowest)
    reach = reach.at[0].set(S // 2)
    return reach.astype(jnp.int32)


def block_levels(key, extent, pieces, smallest, high):
    level = 1.0
    for axis_at, blocks in pieces:
        steps = jax.random.uniform(jax.random.fold_in(jax.random.fold_in(key, 6), axis_at), (blocks,), jnp.float32, smallest / len(pieces), high / len(pieces))
        level = level * jnp.repeat(jnp.exp(steps), extent[axis_at] // blocks).reshape((-1,) + (1,) * (len(extent) - 1 - axis_at))
    return level


def scatter_about(stream_key, extent, scale, limit, cuts=(), kind=jnp.bfloat16):
    gain = block_levels(stream_key, extent, cuts, -0.22, 0.18) if cuts else 1.0
    drawn = jax.random.normal(stream_key, extent, jnp.float32) * scale * gain
    return jnp.minimum(jnp.maximum(drawn, -limit), limit).astype(kind)


def setup_inputs(seed: int = 0, part: int = 0) -> dict:
    key_list = jax.random.split(jax.random.key(seed), 7)
    own_keys = jax.random.split(jax.random.fold_in(key_list[6], part), 7)
    queries = draw_queries(jax.random.fold_in(jax.random.fold_in(key_list[6], part), 71), part)
    keys = draw_keys(jax.random.fold_in(jax.random.fold_in(key_list[6], part), 71), part)
    values = scatter_about(own_keys[2], (FRAMES, S, HEADS * HEAD), 1.0, 6.0, ((0, 4), (2, 4)))
    band_table = draw_band_table(jax.random.fold_in(key_list[6], 71), part)
    windows = draw_windows(jax.random.fold_in(key_list[6], 71), part)
    out_weight = scatter_about(key_list[5], (HEADS * HEAD, D), (HEADS * HEAD) ** -0.5, 0.109375, ((0, 4),))
    return {"queries": queries, "keys": keys, "values": values, "band_table": band_table, "windows": windows, "out_weight": out_weight}


def reference(queries, keys, values, band_table, windows, out_weight):
    heads = HEADS
    scale = HEAD ** -0.5
    key_all = keys.reshape(FRAMES * S, heads, HEAD).astype(jnp.float32)
    value_all = values.reshape(FRAMES * S, heads, HEAD).astype(jnp.float32)
    places = jnp.arange(S, dtype=jnp.int32)
    key_places = jnp.tile(places, FRAMES)
    key_frames = jnp.repeat(jnp.arange(FRAMES, dtype=jnp.int32), S)

    def one_frame(frame):
        query = lax.dynamic_index_in_dim(queries, frame, 0, keepdims=False)
        query = query.reshape(S, heads, HEAD).astype(jnp.float32)
        reach = windows[band_table[frame]]
        allowed = jnp.abs(places[:, None] - key_places[None, :]) <= reach[key_frames][None, :]
        scores = jnp.einsum("phd,qhd->hpq", query, key_all, precision=lax.Precision.HIGHEST) * scale
        masked = jnp.where(allowed[None], scores, jnp.float32(-1e30))
        top = jnp.max(masked, axis=-1, keepdims=True)
        weights = jnp.where(allowed[None], jnp.exp(scores - top), jnp.float32(0.0))
        total = jnp.sum(weights, axis=-1)
        rounded = lax.optimization_barrier(weights.astype(jnp.bfloat16)).astype(jnp.float32)
        numer = jnp.einsum("hpq,qhd->phd", rounded, value_all, precision=lax.Precision.HIGHEST)
        attended = numer / jnp.transpose(total)[:, :, None]
        return attended.reshape(S, heads * HEAD).astype(jnp.bfloat16)

    attended = lax.map(one_frame, jnp.arange(FRAMES, dtype=jnp.int32))
    mixed = jnp.dot(attended.reshape(FRAMES * S, heads * HEAD), out_weight, preferred_element_type=jnp.float32)
    return mixed.astype(jnp.bfloat16).reshape(FRAMES, S, D)
```

```python
import functools

import jax
import jax.numpy as jnp
from jax import lax
from jax.experimental import pallas as pl
from jax.experimental.pallas import tpu as pltpu
from jax.sharding import PartitionSpec as P

HEAD = 128
MESH = pl.DeviceIdType.MESH


def local(queries, keys, values, band_table, windows, out_weight):
    frames, length, width = queries.shape
    heads = width // HEAD
    scale = HEAD ** (-0.5)
    here = lax.axis_index("tm") * frames
    query = queries[0].reshape(length, heads, HEAD)
    places = lax.iota(jnp.int32, length)
    gap = jnp.abs(places[:, None] - places[None, :])

    def absorb(carry, key_frame, value_frame, frame, usable):
        peak, total, numer = carry
        reach = windows[band_table[here, frame]]
        allowed = (gap <= reach)[None] & usable
        scores = (
            jnp.einsum(
                "phd,qhd->hpq",
                query,
                key_frame.reshape(length, heads, HEAD),
                preferred_element_type=jnp.float32,
            )
            * scale
        )
        masked = jnp.where(allowed, scores, jnp.float32(-1e30))
        top = jnp.maximum(peak, jnp.max(masked, axis=-1))
        weights = jnp.where(allowed, jnp.exp(scores - top[:, :, None]), jnp.float32(0.0))
        shrink = jnp.exp(peak - top)
        total = total * shrink + jnp.sum(weights, axis=-1)
        added = jnp.einsum(
            "hpq,qhd->phd",
            weights.astype(jnp.bfloat16),
            value_frame.reshape(length, heads, HEAD),
            preferred_element_type=jnp.float32,
        )
        numer = numer * jnp.transpose(shrink)[:, :, None] + added
        return (top, total, numer)

    carry = (
        jnp.full((heads, length), -1e30, jnp.float32),
        jnp.zeros((heads, length), jnp.float32),
        jnp.zeros((length, heads, HEAD), jnp.float32),
    )
    skipped = -1
    state = carry
    key_part = lax.all_gather(keys, "tm", axis=0, tiled=True)
    value_part = lax.all_gather(values, "tm", axis=0, tiled=True)

    def advance(inner, item):
        key_frame, value_frame, offset = item
        usable = jnp.abs(offset - here) > skipped
        return (absorb(inner, key_frame, value_frame, offset, usable), None)

    state, unused = lax.scan(
        advance, state, (key_part, value_part, lax.iota(jnp.int32, key_part.shape[0]))
    )
    carry = state
    peak, total, numer = carry
    attended = (
        (numer / jnp.transpose(total)[:, :, None]).astype(jnp.bfloat16).reshape(length, width)
    )
    mixed = lax.psum_scatter(
        jnp.dot(attended, out_weight, preferred_element_type=jnp.float32).astype(jnp.bfloat16),
        ("head", "sub"),
        scatter_dimension=0,
        tiled=True,
    )
    return mixed[None]


def fused_kernel(
    n, chunks, q_hbm, k_hbm, v_hbm, band, windows, w_hbm, out_ref,
    buf, weight, done, att, send_a, recv_a, send_b, recv_b, acc,
    in_send, in_recv, back_send, back_recv, a_send, a_recv, b_send, b_recv, w_sem,
):
    frame = lax.axis_index("tm")
    row = lax.axis_index("head")
    core = lax.axis_index("sub")
    length = q_hbm.shape[1]
    heads = 2 * n - 2
    owner = [(h + 1) // 2 for h in range(heads)]
    slot = [1 if h > 0 and h % 2 == 0 else 0 for h in range(heads)]
    scale = HEAD ** (-0.5)

    barrier = pltpu.get_barrier_semaphore()
    for step in range(1, n):
        pl.semaphore_signal(
            barrier, inc=1, device_id={"tm": lax.rem(frame + step, n)}, device_id_type=MESH
        )
    pl.semaphore_signal(barrier, inc=1, device_id={"head": 1 - row}, device_id_type=MESH)
    pl.semaphore_signal(barrier, inc=1, device_id={"sub": 1 - core}, device_id_type=MESH)
    pl.semaphore_wait(barrier, n + 1)

    sources = (q_hbm, k_hbm, v_hbm)
    order = [h for h in range(heads) if slot[h] == 0] + [h for h in range(heads) if slot[h] == 1]

    def outgoing(h, a):
        return pltpu.make_async_remote_copy(
            src_ref=sources[a].at[0, :, h * HEAD : (h + 1) * HEAD],
            dst_ref=buf.at[slot[h], a, frame],
            send_sem=in_send.at[h, a],
            recv_sem=in_recv.at[slot[h], a, frame],
            device_id={"tm": owner[h]},
            device_id_type=MESH,
        )

    for h in order:

        @pl.when(frame != owner[h])
        def _():
            for a in range(3):
                outgoing(h, a).start()

        @pl.when(frame == owner[h])
        def _():
            for a in range(3):
                pltpu.make_async_copy(
                    sources[a].at[0, :, h * HEAD : (h + 1) * HEAD],
                    buf.at[slot[h], a, frame],
                    in_recv.at[slot[h], a, frame],
                ).start()

    load_weight = pltpu.make_async_copy(w_hbm, weight, w_sem)
    load_weight.start()

    gap = jnp.abs(
        lax.broadcasted_iota(jnp.int32, (length, length), 0)
        - lax.broadcasted_iota(jnp.int32, (length, length), 1)
    )

    def returning(s, h, i):
        return pltpu.make_async_remote_copy(
            src_ref=done.at[s, i],
            dst_ref=att.at[:, pl.ds(pl.multiple_of(h * HEAD, HEAD), HEAD)],
            send_sem=back_send.at[s, i],
            recv_sem=back_recv.at[h],
            device_id={"tm": i},
            device_id_type=MESH,
        )

    def attend(s, h):
        for j in range(n):
            for a in range(3):
                pltpu.make_async_copy(buf.at[s, a, j], buf.at[s, a, j], in_recv.at[s, a, j]).wait()

        def one(step, carry):
            i = lax.rem(frame + 1 + step, n)
            query = buf[s, 0, i]
            parts = []
            top = None
            for j in range(n):
                score = lax.dot_general(
                    query, buf[s, 1, j], (((1,), (1,)), ((), ())),
                    preferred_element_type=jnp.float32,
                ) * scale
                score = jnp.where(gap <= windows[band[i, j]], score, jnp.float32(-1e30))
                peak = jnp.max(score, axis=-1, keepdims=True)
                top = peak if top is None else jnp.maximum(top, peak)
                parts.append(score)
            total = None
            numer = None
            for j in range(n):
                part = jnp.exp(parts[j] - top)
                added = jnp.sum(part, axis=-1, keepdims=True)
                product = jnp.dot(
                    part.astype(jnp.bfloat16), buf[s, 2, j], preferred_element_type=jnp.float32
                )
                total = added if total is None else total + added
                numer = product if numer is None else numer + product
            result = (numer / total).astype(jnp.bfloat16)

            @pl.when(i != frame)
            def _():
                done[s, i] = result
                returning(s, h, i).start()

            @pl.when(i == frame)
            def _():
                att[:, pl.ds(pl.multiple_of(h * HEAD, HEAD), HEAD)] = result

            return carry

        lax.fori_loop(0, n, one, 0)

    first = 2 * frame - (frame + n - 1) // n
    second = 2 * frame
    both = jnp.logical_and(frame > 0, frame < n - 1)
    attend(0, first)

    @pl.when(both)
    def _():
        attend(1, second)

    load_weight.wait()
    for h in range(heads):

        @pl.when(frame != owner[h])
        def _():
            here = att.at[:, h * HEAD : (h + 1) * HEAD]
            pltpu.make_async_copy(here, here, back_recv.at[h]).wait()

    block = length // 4
    width = weight.shape[1] // chunks

    def rows(who):
        return jnp.concatenate(
            [
                att[pl.ds(pl.multiple_of(r * 2 * block + who * block, block), block), :]
                for r in (row, 1 - row)
            ],
            axis=0,
        )

    def give_a(c):
        return pltpu.make_async_remote_copy(
            src_ref=send_a.at[c], dst_ref=recv_a.at[c],
            send_sem=a_send.at[c], recv_sem=a_recv.at[c],
            device_id={"sub": 1 - core}, device_id_type=MESH,
        )

    def give_b(c):
        return pltpu.make_async_remote_copy(
            src_ref=send_b.at[c], dst_ref=recv_b.at[c],
            send_sem=b_send.at[c], recv_sem=b_recv.at[c],
            device_id={"head": 1 - row}, device_id_type=MESH,
        )

    theirs = rows(1 - core)
    for c in range(chunks):
        send_a[c] = jnp.dot(
            theirs, weight[:, c * width : (c + 1) * width], preferred_element_type=jnp.float32
        ).astype(jnp.bfloat16)
        give_a(c).start()
    mine = rows(core)
    for c in range(chunks):
        own = jnp.dot(
            mine, weight[:, c * width : (c + 1) * width], preferred_element_type=jnp.float32
        )
        give_a(c).wait_recv()
        own = own + recv_a[c].astype(jnp.float32)
        send_b[c] = own[block:].astype(jnp.bfloat16)
        give_b(c).start()
        acc[c] = own[:block]
    for c in range(chunks):
        give_b(c).wait_recv()
        out_ref[:, c * width : (c + 1) * width] = (
            acc[c] + recv_b[c].astype(jnp.float32)
        ).astype(jnp.bfloat16)

    for c in range(chunks):
        give_a(c).wait_send()
        give_b(c).wait_send()
    for h in range(heads):

        @pl.when(frame != owner[h])
        def _():
            for a in range(3):
                outgoing(h, a).wait_send()

    for i in range(n):

        @pl.when(i != frame)
        def _():
            returning(0, first, i).wait_send()

        @pl.when(jnp.logical_and(both, i != frame))
        def _():
            returning(1, second, i).wait_send()


def fused(n, queries, keys, values, band_table, windows, out_weight):
    length, width = queries.shape[1:]
    columns = out_weight.shape[1]
    heads = width // HEAD
    block = length // 4
    chunks = 4
    part = columns // chunks
    anywhere = pl.BlockSpec(memory_space=pl.ANY)
    scalar = pl.BlockSpec(memory_space=pltpu.SMEM)
    dma = pltpu.SemaphoreType.DMA
    mixed = pl.pallas_call(
        functools.partial(fused_kernel, n, chunks),
        out_shape=jax.ShapeDtypeStruct((block, columns), jnp.bfloat16),
        in_specs=[anywhere, anywhere, anywhere, scalar, scalar, anywhere],
        out_specs=pl.BlockSpec(memory_space=pltpu.VMEM),
        scratch_shapes=[
            pltpu.VMEM((2, 3, n, length, HEAD), jnp.bfloat16),
            pltpu.VMEM(out_weight.shape, jnp.bfloat16),
            pltpu.VMEM((2, n, length, HEAD), jnp.bfloat16),
            pltpu.VMEM((length, width), jnp.bfloat16),
            pltpu.VMEM((chunks, 2 * block, part), jnp.bfloat16),
            pltpu.VMEM((chunks, 2 * block, part), jnp.bfloat16),
            pltpu.VMEM((chunks, block, part), jnp.bfloat16),
            pltpu.VMEM((chunks, block, part), jnp.bfloat16),
            pltpu.VMEM((chunks, block, part), jnp.float32),
            dma((heads, 3)),
            dma((2, 3, n)),
            dma((2, n)),
            dma((heads,)),
            dma((chunks,)),
            dma((chunks,)),
            dma((chunks,)),
            dma((chunks,)),
            dma,
        ],
        compiler_params=pltpu.CompilerParams(
            collective_id=0, has_side_effects=True, vmem_limit_bytes=40 * 1024 * 1024
        ),
    )(queries, keys, values, band_table, windows, out_weight)
    return mixed[None]


def solution(mesh):
    n = mesh.shape["tm"]

    def step(queries, keys, values, band_table, windows, out_weight):
        paired = mesh.shape["head"] == 2 and mesh.shape["sub"] == 2
        if n > 2 and paired and queries.shape[0] == 1 and queries.shape[2] == (2 * n - 2) * HEAD:
            return fused(n, queries, keys, values, band_table, windows, out_weight)
        return local(queries, keys, values, band_table, windows, out_weight)

    return jax.shard_map(
        step,
        mesh=mesh,
        in_specs=(
            P(("clip", "tm"), None, ("head", "sub")),
            P(("clip", "tm"), None, ("head", "sub")),
            P(("clip", "tm"), None, ("head", "sub")),
            P(),
            P(),
            P(("head", "sub"), None),
        ),
        out_specs=P(("clip", "tm"), ("head", "sub"), None),
        check_vma=False,
    )
```

```python
import functools

import jax
import jax.numpy as jnp
from jax import lax
from jax.experimental import pallas as pl
from jax.experimental.pallas import tpu as pltpu
from jax.sharding import PartitionSpec as P

HEAD = 128
MESH = pl.DeviceIdType.MESH


def local(queries, keys, values, band_table, windows, out_weight):
    frames, length, width = queries.shape
    heads = width // HEAD
    scale = HEAD ** (-0.5)
    here = lax.axis_index("tm") * frames
    query = queries[0].reshape(length, heads, HEAD)
    places = lax.iota(jnp.int32, length)
    gap = jnp.abs(places[:, None] - places[None, :])

    def absorb(carry, key_frame, value_frame, frame, usable):
        peak, total, numer = carry
        reach = windows[band_table[here, frame]]
        allowed = (gap <= reach)[None] & usable
        scores = (
            jnp.einsum(
                "phd,qhd->hpq",
                query,
                key_frame.reshape(length, heads, HEAD),
                preferred_element_type=jnp.float32,
            )
            * scale
        )
        masked = jnp.where(allowed, scores, jnp.float32(-1e30))
        top = jnp.maximum(peak, jnp.max(masked, axis=-1))
        weights = jnp.where(allowed, jnp.exp(scores - top[:, :, None]), jnp.float32(0.0))
        shrink = jnp.exp(peak - top)
        total = total * shrink + jnp.sum(weights, axis=-1)
        added = jnp.einsum(
            "hpq,qhd->phd",
            weights.astype(jnp.bfloat16),
            value_frame.reshape(length, heads, HEAD),
            preferred_element_type=jnp.float32,
        )
        numer = numer * jnp.transpose(shrink)[:, :, None] + added
        return (top, total, numer)

    carry = (
        jnp.full((heads, length), -1e30, jnp.float32),
        jnp.zeros((heads, length), jnp.float32),
        jnp.zeros((length, heads, HEAD), jnp.float32),
    )
    skipped = -1
    state = carry
    key_part = lax.all_gather(keys, "tm", axis=0, tiled=True)
    value_part = lax.all_gather(values, "tm", axis=0, tiled=True)

    def advance(inner, item):
        key_frame, value_frame, offset = item
        usable = jnp.abs(offset - here) > skipped
        return (absorb(inner, key_frame, value_frame, offset, usable), None)

    state, unused = lax.scan(
        advance, state, (key_part, value_part, lax.iota(jnp.int32, key_part.shape[0]))
    )
    carry = state
    peak, total, numer = carry
    attended = (
        (numer / jnp.transpose(total)[:, :, None]).astype(jnp.bfloat16).reshape(length, width)
    )
    mixed = lax.psum_scatter(
        jnp.dot(attended, out_weight, preferred_element_type=jnp.float32).astype(jnp.bfloat16),
        ("head", "sub"),
        scatter_dimension=0,
        tiled=True,
    )
    return mixed[None]


def fused_kernel(
    n, pieces, chunks, q_hbm, k_hbm, v_hbm, band_hbm, windows_hbm, w_hbm, out_ref,
    band, windows, buf, weight, done, att, send_a, recv_a, send_b, recv_b, acc, own,
    in_send, in_recv, back_send, back_recv, a_send, a_recv, b_send, b_recv, w_sem, table_sem,
):
    frame = lax.axis_index("tm")
    row = lax.axis_index("head")
    core = lax.axis_index("sub")
    length = q_hbm.shape[1]
    heads = 2 * n - 2
    owner = [(h + 1) // 2 for h in range(heads)]
    slot = [1 if h > 0 and h % 2 == 0 else 0 for h in range(heads)]
    scale = HEAD ** (-0.5)

    barrier = pltpu.get_barrier_semaphore()
    for step in range(1, n):
        pl.semaphore_signal(
            barrier, inc=1, device_id={"tm": lax.rem(frame + step, n)}, device_id_type=MESH
        )
    pl.semaphore_signal(barrier, inc=1, device_id={"head": 1 - row}, device_id_type=MESH)
    pl.semaphore_signal(barrier, inc=1, device_id={"sub": 1 - core}, device_id_type=MESH)
    pl.semaphore_wait(barrier, n + 1)

    sources = (q_hbm, k_hbm, v_hbm)
    low = frame < n // 2

    def outgoing(h, a):
        return pltpu.make_async_remote_copy(
            src_ref=sources[a].at[0, :, h * HEAD : (h + 1) * HEAD],
            dst_ref=buf.at[slot[h], a, frame],
            send_sem=in_send.at[h, a],
            recv_sem=in_recv.at[slot[h], a, frame],
            device_id={"tm": owner[h]},
            device_id_type=MESH,
        )

    def send_head(h, ready):
        @pl.when(jnp.logical_and(ready, frame != owner[h]))
        def _():
            for a in range(3):
                outgoing(h, a).start()

    for s in range(2):
        below = [h for h in range(heads) if slot[h] == s and owner[h] < n // 2]
        above = [h for h in reversed(range(heads)) if slot[h] == s and owner[h] >= n // 2]
        for h in above:
            send_head(h, low)
        for h in below:
            send_head(h, frame >= 0)
        for h in above:
            send_head(h, jnp.logical_not(low))
    for h in range(heads):

        @pl.when(frame == owner[h])
        def _():
            for a in range(3):
                pltpu.make_async_copy(
                    sources[a].at[0, :, h * HEAD : (h + 1) * HEAD],
                    buf.at[slot[h], a, frame],
                    in_recv.at[slot[h], a, frame],
                ).start()

    load_weight = pltpu.make_async_copy(w_hbm, weight, w_sem)
    load_weight.start()
    tables = (
        pltpu.make_async_copy(band_hbm, band, table_sem.at[0]),
        pltpu.make_async_copy(windows_hbm, windows, table_sem.at[1]),
    )
    for table in tables:
        table.start()

    for table in tables:
        table.wait()
    block = length // 4
    slab = block // pieces
    height = 4 * slab
    spot = lax.broadcasted_iota(jnp.int32, (height, length), 0)
    spot = (spot // slab) * block + lax.rem(spot, slab)
    spot = spot - lax.broadcasted_iota(jnp.int32, (height, length), 1)

    def returning(s, h, p, i):
        return pltpu.make_async_remote_copy(
            src_ref=done.at[s, p, i],
            dst_ref=att.at[p, :, pl.ds(pl.multiple_of(h * HEAD, HEAD), HEAD)],
            send_sem=back_send.at[s, p, i],
            recv_sem=back_recv.at[p, h],
            device_id={"tm": i},
            device_id_type=MESH,
        )

    def arrive(s):
        for j in range(n):
            for a in range(3):
                pltpu.make_async_copy(buf.at[s, a, j], buf.at[s, a, j], in_recv.at[s, a, j]).wait()

    def attend(s, h, p):
        gap = jnp.abs(spot + p * slab)

        def one(step, carry):
            i = lax.rem(frame + 1 + step, n)
            query = jnp.concatenate(
                [buf[s, 0, i, b * block + p * slab : b * block + (p + 1) * slab, :] for b in range(4)],
                axis=0,
            )
            parts = []
            top = None
            for j in range(n):
                score = lax.dot_general(
                    query, buf[s, 1, j], (((1,), (1,)), ((), ())),
                    preferred_element_type=jnp.float32,
                ) * scale
                score = jnp.where(gap <= windows[band[i, j]], score, jnp.float32(-1e30))
                peak = jnp.max(score, axis=-1, keepdims=True)
                top = peak if top is None else jnp.maximum(top, peak)
                parts.append(score)
            total = None
            numer = None
            for j in range(n):
                part = jnp.exp(parts[j] - top)
                added = jnp.sum(part, axis=-1, keepdims=True)
                product = jnp.dot(
                    part.astype(jnp.bfloat16), buf[s, 2, j], preferred_element_type=jnp.float32
                )
                total = added if total is None else total + added
                numer = product if numer is None else numer + product
            result = (numer / total).astype(jnp.bfloat16)

            @pl.when(i != frame)
            def _():
                done[s, p, i] = result
                returning(s, h, p, i).start()

            @pl.when(i == frame)
            def _():
                att[p, :, pl.ds(pl.multiple_of(h * HEAD, HEAD), HEAD)] = result

            return carry

        lax.fori_loop(0, n, one, 0)

    first = 2 * frame - (frame + n - 1) // n
    second = 2 * frame
    both = jnp.logical_and(frame > 0, frame < n - 1)
    arrive(0)
    attend(0, first, 0)

    @pl.when(both)
    def _():
        arrive(1)
        attend(1, second, 0)

    for p in range(1, pieces):
        attend(0, first, p)

        @pl.when(both)
        def _():
            attend(1, second, p)

    load_weight.wait()
    width = weight.shape[1] // chunks

    def rows(p, who):
        return jnp.concatenate(
            [
                att[p, pl.ds(pl.multiple_of((r * 2 + who) * slab, slab), slab), :]
                for r in (row, 1 - row)
            ],
            axis=0,
        )

    def give_a(p, c):
        return pltpu.make_async_remote_copy(
            src_ref=send_a.at[p, c], dst_ref=recv_a.at[p, c],
            send_sem=a_send.at[p, c], recv_sem=a_recv.at[p, c],
            device_id={"sub": 1 - core}, device_id_type=MESH,
        )

    def give_b(p, c):
        return pltpu.make_async_remote_copy(
            src_ref=send_b.at[p, c], dst_ref=recv_b.at[p, c],
            send_sem=b_send.at[p, c], recv_sem=b_recv.at[p, c],
            device_id={"head": 1 - row}, device_id_type=MESH,
        )

    for p in range(pieces):
        for h in range(heads):

            @pl.when(frame != owner[h])
            def _():
                here = att.at[p, :, h * HEAD : (h + 1) * HEAD]
                pltpu.make_async_copy(here, here, back_recv.at[p, h]).wait()

        tokens = jnp.concatenate([rows(p, 1 - core), rows(p, core)], axis=0)
        for c in range(chunks):
            share = jnp.dot(
                tokens, weight[:, c * width : (c + 1) * width], preferred_element_type=jnp.float32
            )
            send_a[p, c] = share[: 2 * slab].astype(jnp.bfloat16)
            give_a(p, c).start()
            own[c] = share[2 * slab :]
        for c in range(chunks):
            give_a(p, c).wait_recv()
            both_cores = own[c] + recv_a[p, c].astype(jnp.float32)
            send_b[p, c] = both_cores[slab:].astype(jnp.bfloat16)
            give_b(p, c).start()
            acc[p, c] = both_cores[:slab]

    for p in range(pieces):
        for c in range(chunks):
            give_b(p, c).wait_recv()
            out_ref[p * slab : (p + 1) * slab, c * width : (c + 1) * width] = (
                acc[p, c] + recv_b[p, c].astype(jnp.float32)
            ).astype(jnp.bfloat16)

    for p in range(pieces):
        for c in range(chunks):
            give_a(p, c).wait_send()
            give_b(p, c).wait_send()
    for h in range(heads):

        @pl.when(frame != owner[h])
        def _():
            for a in range(3):
                outgoing(h, a).wait_send()

    for i in range(n):

        @pl.when(i != frame)
        def _():
            for p in range(pieces):
                returning(0, first, p, i).wait_send()

        @pl.when(jnp.logical_and(both, i != frame))
        def _():
            for p in range(pieces):
                returning(1, second, p, i).wait_send()


def fused(n, queries, keys, values, band_table, windows, out_weight):
    length, width = queries.shape[1:]
    columns = out_weight.shape[1]
    heads = width // HEAD
    block = length // 4
    chunks = 4
    pieces = 2
    slab = block // pieces
    part = columns // chunks
    anywhere = pl.BlockSpec(memory_space=pl.ANY)
    dma = pltpu.SemaphoreType.DMA
    mixed = pl.pallas_call(
        functools.partial(fused_kernel, n, pieces, chunks),
        out_shape=jax.ShapeDtypeStruct((block, columns), jnp.bfloat16),
        in_specs=[anywhere] * 6,
        out_specs=pl.BlockSpec(memory_space=pltpu.VMEM),
        scratch_shapes=[
            pltpu.SMEM(band_table.shape, jnp.int32),
            pltpu.SMEM(windows.shape, jnp.int32),
            pltpu.VMEM((2, 3, n, length, HEAD), jnp.bfloat16),
            pltpu.VMEM(out_weight.shape, jnp.bfloat16),
            pltpu.VMEM((2, pieces, n, 4 * slab, HEAD), jnp.bfloat16),
            pltpu.VMEM((pieces, 4 * slab, width), jnp.bfloat16),
            pltpu.VMEM((pieces, chunks, 2 * slab, part), jnp.bfloat16),
            pltpu.VMEM((pieces, chunks, 2 * slab, part), jnp.bfloat16),
            pltpu.VMEM((pieces, chunks, slab, part), jnp.bfloat16),
            pltpu.VMEM((pieces, chunks, slab, part), jnp.bfloat16),
            pltpu.VMEM((pieces, chunks, slab, part), jnp.float32),
            pltpu.VMEM((chunks, 2 * slab, part), jnp.float32),
            dma((heads, 3)),
            dma((2, 3, n)),
            dma((2, pieces, n)),
            dma((pieces, heads)),
            dma((pieces, chunks)),
            dma((pieces, chunks)),
            dma((pieces, chunks)),
            dma((pieces, chunks)),
            dma,
            dma((2,)),
        ],
        compiler_params=pltpu.CompilerParams(
            collective_id=0, has_side_effects=True, vmem_limit_bytes=60 * 1024 * 1024
        ),
    )(queries, keys, values, band_table, windows, out_weight)
    return mixed[None]


def solution(mesh):
    n = mesh.shape["tm"]

    def step(queries, keys, values, band_table, windows, out_weight):
        paired = mesh.shape["head"] == 2 and mesh.shape["sub"] == 2
        if n > 2 and paired and queries.shape[0] == 1 and queries.shape[2] == (2 * n - 2) * HEAD:
            return fused(n, queries, keys, values, band_table, windows, out_weight)
        return local(queries, keys, values, band_table, windows, out_weight)

    return jax.shard_map(
        step,
        mesh=mesh,
        in_specs=(
            P(("clip", "tm"), None, ("head", "sub")),
            P(("clip", "tm"), None, ("head", "sub")),
            P(("clip", "tm"), None, ("head", "sub")),
            P(),
            P(),
            P(("head", "sub"), None),
        ),
        out_specs=P(("clip", "tm"), ("head", "sub"), None),
        check_vma=False,
    )
```

```python
import functools

import jax
import jax.numpy as jnp
from jax import lax
from jax.experimental import pallas as pl
from jax.experimental.pallas import tpu as pltpu
from jax.sharding import PartitionSpec as P

HEAD = 128
MESH = pl.DeviceIdType.MESH


def local(queries, keys, values, band_table, windows, out_weight):
    frames, length, width = queries.shape
    heads = width // HEAD
    scale = HEAD ** (-0.5)
    here = lax.axis_index("tm") * frames
    query = queries[0].reshape(length, heads, HEAD)
    places = lax.iota(jnp.int32, length)
    gap = jnp.abs(places[:, None] - places[None, :])

    def absorb(carry, key_frame, value_frame, frame, usable):
        peak, total, numer = carry
        reach = windows[band_table[here, frame]]
        allowed = (gap <= reach)[None] & usable
        scores = (
            jnp.einsum(
                "phd,qhd->hpq",
                query,
                key_frame.reshape(length, heads, HEAD),
                preferred_element_type=jnp.float32,
            )
            * scale
        )
        masked = jnp.where(allowed, scores, jnp.float32(-1e30))
        top = jnp.maximum(peak, jnp.max(masked, axis=-1))
        weights = jnp.where(allowed, jnp.exp(scores - top[:, :, None]), jnp.float32(0.0))
        shrink = jnp.exp(peak - top)
        total = total * shrink + jnp.sum(weights, axis=-1)
        added = jnp.einsum(
            "hpq,qhd->phd",
            weights.astype(jnp.bfloat16),
            value_frame.reshape(length, heads, HEAD),
            preferred_element_type=jnp.float32,
        )
        numer = numer * jnp.transpose(shrink)[:, :, None] + added
        return (top, total, numer)

    carry = (
        jnp.full((heads, length), -1e30, jnp.float32),
        jnp.zeros((heads, length), jnp.float32),
        jnp.zeros((length, heads, HEAD), jnp.float32),
    )
    skipped = -1
    state = carry
    key_part = lax.all_gather(keys, "tm", axis=0, tiled=True)
    value_part = lax.all_gather(values, "tm", axis=0, tiled=True)

    def advance(inner, item):
        key_frame, value_frame, offset = item
        usable = jnp.abs(offset - here) > skipped
        return (absorb(inner, key_frame, value_frame, offset, usable), None)

    state, unused = lax.scan(
        advance, state, (key_part, value_part, lax.iota(jnp.int32, key_part.shape[0]))
    )
    carry = state
    peak, total, numer = carry
    attended = (
        (numer / jnp.transpose(total)[:, :, None]).astype(jnp.bfloat16).reshape(length, width)
    )
    mixed = lax.psum_scatter(
        jnp.dot(attended, out_weight, preferred_element_type=jnp.float32).astype(jnp.bfloat16),
        ("head", "sub"),
        scatter_dimension=0,
        tiled=True,
    )
    return mixed[None]


def fused_kernel(
    n, pieces, chunks, q_hbm, k_hbm, v_hbm, band_hbm, windows_hbm, w_hbm, out_ref,
    band, windows, asked, buf, weight, done, att, send_a, recv_a, send_b, recv_b, acc, own,
    in_send, in_recv, back_send, back_recv, a_send, a_recv, b_send, b_recv, w_sem, table_sem,
):
    frame = lax.axis_index("tm")
    row = lax.axis_index("head")
    core = lax.axis_index("sub")
    length = k_hbm.shape[1]
    block = length // 4
    slab = block // pieces
    heads = 2 * n - 2
    owner = [(h + 1) // 2 for h in range(heads)]
    slot = [1 if h > 0 and h % 2 == 0 else 0 for h in range(heads)]
    scale = HEAD ** (-0.5)

    barrier = pltpu.get_barrier_semaphore()
    for step in range(1, n):
        pl.semaphore_signal(
            barrier, inc=1, device_id={"tm": lax.rem(frame + step, n)}, device_id_type=MESH
        )
    pl.semaphore_signal(barrier, inc=1, device_id={"head": 1 - row}, device_id_type=MESH)
    pl.semaphore_signal(barrier, inc=1, device_id={"sub": 1 - core}, device_id_type=MESH)
    pl.semaphore_wait(barrier, n + 1)

    low = frame < n // 2

    def ends(h, a):
        columns = slice(h * HEAD, (h + 1) * HEAD)
        if a < 2:
            return (k_hbm, v_hbm)[a].at[0, :, columns], buf.at[slot[h], a, frame]
        p = a - 2
        source = q_hbm.at[:, p * slab : (p + 1) * slab, columns]
        return source, asked.at[slot[h], p, frame]

    def outgoing(h, a):
        source, target = ends(h, a)
        return pltpu.make_async_remote_copy(
            src_ref=source,
            dst_ref=target,
            send_sem=in_send.at[h, a],
            recv_sem=in_recv.at[slot[h], a, frame],
            device_id={"tm": owner[h]},
            device_id_type=MESH,
        )

    def send_head(h, ready, which):
        @pl.when(jnp.logical_and(ready, frame != owner[h]))
        def _():
            for a in which:
                outgoing(h, a).start()

    def send_slot(s, which):
        below = [h for h in range(heads) if slot[h] == s and owner[h] < n // 2]
        above = [h for h in reversed(range(heads)) if slot[h] == s and owner[h] >= n // 2]
        for h in above:
            send_head(h, low, which)
        for h in below:
            send_head(h, frame >= 0, which)
        for h in above:
            send_head(h, jnp.logical_not(low), which)

    send_slot(0, (0, 1))
    send_slot(1, (0, 1))
    send_slot(0, (2,))
    send_slot(1, (2,))
    for p in range(1, pieces):
        send_slot(0, (2 + p,))
        send_slot(1, (2 + p,))
    for h in range(heads):

        @pl.when(frame == owner[h])
        def _():
            for a in range(2 + pieces):
                source, target = ends(h, a)
                pltpu.make_async_copy(source, target, in_recv.at[slot[h], a, frame]).start()

    load_weight = pltpu.make_async_copy(w_hbm, weight, w_sem)
    load_weight.start()
    tables = (
        pltpu.make_async_copy(band_hbm, band, table_sem.at[0]),
        pltpu.make_async_copy(windows_hbm, windows, table_sem.at[1]),
    )
    for table in tables:
        table.start()

    for table in tables:
        table.wait()
    height = 4 * slab
    spot = lax.broadcasted_iota(jnp.int32, (height, length), 0)
    spot = (spot // slab) * block + lax.rem(spot, slab)
    spot = spot - lax.broadcasted_iota(jnp.int32, (height, length), 1)

    def returning(s, h, p, i):
        return pltpu.make_async_remote_copy(
            src_ref=done.at[s, p, i],
            dst_ref=att.at[p, :, pl.ds(pl.multiple_of(h * HEAD, HEAD), HEAD)],
            send_sem=back_send.at[s, p, i],
            recv_sem=back_recv.at[p, h],
            device_id={"tm": i},
            device_id_type=MESH,
        )

    def arrive(s, p):
        for j in range(n):
            for a in (0, 1) if p == 0 else ():
                pltpu.make_async_copy(buf.at[s, a, j], buf.at[s, a, j], in_recv.at[s, a, j]).wait()
            here = asked.at[s, p, j]
            pltpu.make_async_copy(here, here, in_recv.at[s, 2 + p, j]).wait()

    def attend(s, h, p):
        gap = jnp.abs(spot + p * slab)

        def one(step, carry):
            i = lax.rem(frame + 1 + step, n)
            query = asked[s, p, i].reshape(height, HEAD)
            parts = []
            top = None
            for j in range(n):
                score = lax.dot_general(
                    query, buf[s, 0, j], (((1,), (1,)), ((), ())),
                    preferred_element_type=jnp.float32,
                ) * scale
                score = jnp.where(gap <= windows[band[i, j]], score, jnp.float32(-1e30))
                peak = jnp.max(score, axis=-1, keepdims=True)
                top = peak if top is None else jnp.maximum(top, peak)
                parts.append(score)
            total = None
            numer = None
            for j in range(n):
                part = jnp.exp(parts[j] - top)
                added = jnp.sum(part, axis=-1, keepdims=True)
                product = jnp.dot(
                    part.astype(jnp.bfloat16), buf[s, 1, j], preferred_element_type=jnp.float32
                )
                total = added if total is None else total + added
                numer = product if numer is None else numer + product
            result = (numer / total).astype(jnp.bfloat16)

            @pl.when(i != frame)
            def _():
                done[s, p, i] = result
                returning(s, h, p, i).start()

            @pl.when(i == frame)
            def _():
                att[p, :, pl.ds(pl.multiple_of(h * HEAD, HEAD), HEAD)] = result

            return carry

        lax.fori_loop(0, n, one, 0)

    first = 2 * frame - (frame + n - 1) // n
    second = 2 * frame
    both = jnp.logical_and(frame > 0, frame < n - 1)
    for p in range(pieces):
        arrive(0, p)
        attend(0, first, p)

        @pl.when(both)
        def _():
            arrive(1, p)
            attend(1, second, p)

    load_weight.wait()
    width = weight.shape[1] // chunks

    def rows(p, who):
        return jnp.concatenate(
            [
                att[p, pl.ds(pl.multiple_of((r * 2 + who) * slab, slab), slab), :]
                for r in (row, 1 - row)
            ],
            axis=0,
        )

    def give_a(p, c):
        return pltpu.make_async_remote_copy(
            src_ref=send_a.at[p, c], dst_ref=recv_a.at[p, c],
            send_sem=a_send.at[p, c], recv_sem=a_recv.at[p, c],
            device_id={"sub": 1 - core}, device_id_type=MESH,
        )

    def give_b(p, c):
        return pltpu.make_async_remote_copy(
            src_ref=send_b.at[p, c], dst_ref=recv_b.at[p, c],
            send_sem=b_send.at[p, c], recv_sem=b_recv.at[p, c],
            device_id={"head": 1 - row}, device_id_type=MESH,
        )

    for p in range(pieces):
        for h in range(heads):

            @pl.when(frame != owner[h])
            def _():
                here = att.at[p, :, h * HEAD : (h + 1) * HEAD]
                pltpu.make_async_copy(here, here, back_recv.at[p, h]).wait()

        tokens = jnp.concatenate([rows(p, 1 - core), rows(p, core)], axis=0)
        for c in range(chunks):
            share = jnp.dot(
                tokens, weight[:, c * width : (c + 1) * width], preferred_element_type=jnp.float32
            )
            send_a[p, c] = share[: 2 * slab].astype(jnp.bfloat16)
            give_a(p, c).start()
            own[c] = share[2 * slab :]
        for c in range(chunks):
            give_a(p, c).wait_recv()
            both_cores = own[c] + recv_a[p, c].astype(jnp.float32)
            send_b[p, c] = both_cores[slab:].astype(jnp.bfloat16)
            give_b(p, c).start()
            acc[p, c] = both_cores[:slab]

    for p in range(pieces):
        for c in range(chunks):
            give_b(p, c).wait_recv()
            out_ref[p * slab : (p + 1) * slab, c * width : (c + 1) * width] = (
                acc[p, c] + recv_b[p, c].astype(jnp.float32)
            ).astype(jnp.bfloat16)

    for p in range(pieces):
        for c in range(chunks):
            give_a(p, c).wait_send()
            give_b(p, c).wait_send()
    for h in range(heads):

        @pl.when(frame != owner[h])
        def _():
            for a in range(2 + pieces):
                outgoing(h, a).wait_send()

    for i in range(n):

        @pl.when(i != frame)
        def _():
            for p in range(pieces):
                returning(0, first, p, i).wait_send()

        @pl.when(jnp.logical_and(both, i != frame))
        def _():
            for p in range(pieces):
                returning(1, second, p, i).wait_send()


def fused(n, queries, keys, values, band_table, windows, out_weight):
    length, width = queries.shape[1:]
    columns = out_weight.shape[1]
    heads = width // HEAD
    block = length // 4
    chunks = 4
    pieces = 2
    slab = block // pieces
    part = columns // chunks
    anywhere = pl.BlockSpec(memory_space=pl.ANY)
    dma = pltpu.SemaphoreType.DMA
    mixed = pl.pallas_call(
        functools.partial(fused_kernel, n, pieces, chunks),
        out_shape=jax.ShapeDtypeStruct((block, columns), jnp.bfloat16),
        in_specs=[anywhere] * 6,
        out_specs=pl.BlockSpec(memory_space=pltpu.VMEM),
        scratch_shapes=[
            pltpu.SMEM(band_table.shape, jnp.int32),
            pltpu.SMEM(windows.shape, jnp.int32),
            pltpu.VMEM((2, pieces, n, 4, slab, HEAD), jnp.bfloat16),
            pltpu.VMEM((2, 2, n, length, HEAD), jnp.bfloat16),
            pltpu.VMEM(out_weight.shape, jnp.bfloat16),
            pltpu.VMEM((2, pieces, n, 4 * slab, HEAD), jnp.bfloat16),
            pltpu.VMEM((pieces, 4 * slab, width), jnp.bfloat16),
            pltpu.VMEM((pieces, chunks, 2 * slab, part), jnp.bfloat16),
            pltpu.VMEM((pieces, chunks, 2 * slab, part), jnp.bfloat16),
            pltpu.VMEM((pieces, chunks, slab, part), jnp.bfloat16),
            pltpu.VMEM((pieces, chunks, slab, part), jnp.bfloat16),
            pltpu.VMEM((pieces, chunks, slab, part), jnp.float32),
            pltpu.VMEM((chunks, 2 * slab, part), jnp.float32),
            dma((heads, 2 + pieces)),
            dma((2, 2 + pieces, n)),
            dma((2, pieces, n)),
            dma((pieces, heads)),
            dma((pieces, chunks)),
            dma((pieces, chunks)),
            dma((pieces, chunks)),
            dma((pieces, chunks)),
            dma,
            dma((2,)),
        ],
        compiler_params=pltpu.CompilerParams(
            collective_id=0, has_side_effects=True, vmem_limit_bytes=60 * 1024 * 1024
        ),
    )(queries.reshape(4, block, width), keys, values, band_table, windows, out_weight)
    return mixed[None]


def solution(mesh):
    n = mesh.shape["tm"]

    def step(queries, keys, values, band_table, windows, out_weight):
        paired = mesh.shape["head"] == 2 and mesh.shape["sub"] == 2
        if n > 2 and paired and queries.shape[0] == 1 and queries.shape[2] == (2 * n - 2) * HEAD:
            return fused(n, queries, keys, values, band_table, windows, out_weight)
        return local(queries, keys, values, band_table, windows, out_weight)

    return jax.shard_map(
        step,
        mesh=mesh,
        in_specs=(
            P(("clip", "tm"), None, ("head", "sub")),
            P(("clip", "tm"), None, ("head", "sub")),
            P(("clip", "tm"), None, ("head", "sub")),
            P(),
            P(),
            P(("head", "sub"), None),
        ),
        out_specs=P(("clip", "tm"), ("head", "sub"), None),
        check_vma=False,
    )
```

```python
import functools

import jax
import jax.numpy as jnp
from jax import lax
from jax.experimental import pallas as pl
from jax.experimental.pallas import tpu as pltpu
from jax.sharding import PartitionSpec as P

HEAD = 128
MESH = pl.DeviceIdType.MESH


def local(queries, keys, values, band_table, windows, out_weight):
    frames, length, width = queries.shape
    heads = width // HEAD
    scale = HEAD ** (-0.5)
    here = lax.axis_index("tm") * frames
    query = queries[0].reshape(length, heads, HEAD)
    places = lax.iota(jnp.int32, length)
    gap = jnp.abs(places[:, None] - places[None, :])

    def absorb(carry, key_frame, value_frame, frame, usable):
        peak, total, numer = carry
        reach = windows[band_table[here, frame]]
        allowed = (gap <= reach)[None] & usable
        scores = (
            jnp.einsum(
                "phd,qhd->hpq",
                query,
                key_frame.reshape(length, heads, HEAD),
                preferred_element_type=jnp.float32,
            )
            * scale
        )
        masked = jnp.where(allowed, scores, jnp.float32(-1e30))
        top = jnp.maximum(peak, jnp.max(masked, axis=-1))
        weights = jnp.where(allowed, jnp.exp(scores - top[:, :, None]), jnp.float32(0.0))
        shrink = jnp.exp(peak - top)
        total = total * shrink + jnp.sum(weights, axis=-1)
        added = jnp.einsum(
            "hpq,qhd->phd",
            weights.astype(jnp.bfloat16),
            value_frame.reshape(length, heads, HEAD),
            preferred_element_type=jnp.float32,
        )
        numer = numer * jnp.transpose(shrink)[:, :, None] + added
        return (top, total, numer)

    carry = (
        jnp.full((heads, length), -1e30, jnp.float32),
        jnp.zeros((heads, length), jnp.float32),
        jnp.zeros((length, heads, HEAD), jnp.float32),
    )
    skipped = -1
    state = carry
    key_part = lax.all_gather(keys, "tm", axis=0, tiled=True)
    value_part = lax.all_gather(values, "tm", axis=0, tiled=True)

    def advance(inner, item):
        key_frame, value_frame, offset = item
        usable = jnp.abs(offset - here) > skipped
        return (absorb(inner, key_frame, value_frame, offset, usable), None)

    state, unused = lax.scan(
        advance, state, (key_part, value_part, lax.iota(jnp.int32, key_part.shape[0]))
    )
    carry = state
    peak, total, numer = carry
    attended = (
        (numer / jnp.transpose(total)[:, :, None]).astype(jnp.bfloat16).reshape(length, width)
    )
    mixed = lax.psum_scatter(
        jnp.dot(attended, out_weight, preferred_element_type=jnp.float32).astype(jnp.bfloat16),
        ("head", "sub"),
        scatter_dimension=0,
        tiled=True,
    )
    return mixed[None]


def fused_kernel(
    n, pieces, chunks, q_hbm, k_hbm, v_hbm, band_hbm, windows_hbm, w_hbm, out_ref,
    band, windows, asked, buf, weight, done, att, send_a, recv_a, send_b, recv_b, acc, own,
    in_send, in_recv, back_send, back_recv, a_send, a_recv, b_send, b_recv, w_sem, table_sem,
):
    frame = lax.axis_index("tm")
    row = lax.axis_index("head")
    core = lax.axis_index("sub")
    length = k_hbm.shape[1]
    block = length // 4
    slab = block // pieces
    heads = 2 * n - 2
    owner = [(h + 1) // 2 for h in range(heads)]
    slot = [1 if h > 0 and h % 2 == 0 else 0 for h in range(heads)]
    scale = HEAD ** (-0.5)

    barrier = pltpu.get_barrier_semaphore()
    for step in range(1, n):
        pl.semaphore_signal(
            barrier, inc=1, device_id={"tm": lax.rem(frame + step, n)}, device_id_type=MESH
        )
    pl.semaphore_signal(barrier, inc=1, device_id={"head": 1 - row}, device_id_type=MESH)
    pl.semaphore_signal(barrier, inc=1, device_id={"sub": 1 - core}, device_id_type=MESH)
    pl.semaphore_wait(barrier, n + 1)

    low = frame < n // 2

    def ends(h, a):
        columns = slice(h * HEAD, (h + 1) * HEAD)
        if a < 2:
            return (k_hbm, v_hbm)[a].at[0, :, columns], buf.at[slot[h], a, frame]
        p = a - 2
        source = q_hbm.at[:, p * slab : (p + 1) * slab, columns]
        return source, asked.at[slot[h], p, frame]

    def outgoing(h, a):
        source, target = ends(h, a)
        return pltpu.make_async_remote_copy(
            src_ref=source,
            dst_ref=target,
            send_sem=in_send.at[h, a],
            recv_sem=in_recv.at[slot[h], a, frame],
            device_id={"tm": owner[h]},
            device_id_type=MESH,
        )

    def send_head(h, ready, which):
        @pl.when(jnp.logical_and(ready, frame != owner[h]))
        def _():
            for a in which:
                outgoing(h, a).start()

    def send_slot(s, which):
        below = [h for h in range(heads) if slot[h] == s and owner[h] < n // 2]
        above = [h for h in reversed(range(heads)) if slot[h] == s and owner[h] >= n // 2]
        for h in above:
            send_head(h, low, which)
        for h in below:
            send_head(h, frame >= 0, which)
        for h in above:
            send_head(h, jnp.logical_not(low), which)

    send_slot(0, (0, 1, 2))
    send_slot(1, (0, 1, 2))
    for p in range(1, pieces):
        send_slot(0, (2 + p,))
        send_slot(1, (2 + p,))
    for h in range(heads):

        @pl.when(frame == owner[h])
        def _():
            for a in range(2 + pieces):
                source, target = ends(h, a)
                pltpu.make_async_copy(source, target, in_recv.at[slot[h], a, frame]).start()

    load_weight = pltpu.make_async_copy(w_hbm, weight, w_sem)
    load_weight.start()
    tables = (
        pltpu.make_async_copy(band_hbm, band, table_sem.at[0]),
        pltpu.make_async_copy(windows_hbm, windows, table_sem.at[1]),
    )
    for table in tables:
        table.start()

    for table in tables:
        table.wait()
    height = 4 * slab
    spot = lax.broadcasted_iota(jnp.int32, (height, length), 0)
    spot = (spot // slab) * block + lax.rem(spot, slab)
    spot = spot - lax.broadcasted_iota(jnp.int32, (height, length), 1)

    def returning(s, h, p, i):
        return pltpu.make_async_remote_copy(
            src_ref=done.at[s, p, i],
            dst_ref=att.at[p, :, pl.ds(pl.multiple_of(h * HEAD, HEAD), HEAD)],
            send_sem=back_send.at[s, p, i],
            recv_sem=back_recv.at[p, h],
            device_id={"tm": i},
            device_id_type=MESH,
        )

    def arrive(s, p):
        for j in range(n):
            for a in (0, 1) if p == 0 else ():
                pltpu.make_async_copy(buf.at[s, a, j], buf.at[s, a, j], in_recv.at[s, a, j]).wait()
            here = asked.at[s, p, j]
            pltpu.make_async_copy(here, here, in_recv.at[s, 2 + p, j]).wait()

    def attend(s, h, p):
        gap = jnp.abs(spot + p * slab)

        def one(step, carry):
            i = lax.rem(frame + 1 + step, n)
            query = asked[s, p, i].reshape(height, HEAD)
            parts = []
            top = None
            for j in range(n):
                score = lax.dot_general(
                    query, buf[s, 0, j], (((1,), (1,)), ((), ())),
                    preferred_element_type=jnp.float32,
                ) * scale
                score = jnp.where(gap <= windows[band[i, j]], score, jnp.float32(-1e30))
                peak = jnp.max(score, axis=-1, keepdims=True)
                top = peak if top is None else jnp.maximum(top, peak)
                parts.append(score)
            total = None
            numer = None
            for j in range(n):
                part = jnp.exp(parts[j] - top)
                added = jnp.sum(part, axis=-1, keepdims=True)
                product = jnp.dot(
                    part.astype(jnp.bfloat16), buf[s, 1, j], preferred_element_type=jnp.float32
                )
                total = added if total is None else total + added
                numer = product if numer is None else numer + product
            result = (numer / total).astype(jnp.bfloat16)

            @pl.when(i != frame)
            def _():
                done[s, p, i] = result
                returning(s, h, p, i).start()

            @pl.when(i == frame)
            def _():
                att[p, :, pl.ds(pl.multiple_of(h * HEAD, HEAD), HEAD)] = result

            return carry

        lax.fori_loop(0, n, one, 0)

    first = 2 * frame - (frame + n - 1) // n
    second = 2 * frame
    both = jnp.logical_and(frame > 0, frame < n - 1)
    for p in range(pieces):
        arrive(0, p)
        attend(0, first, p)

        @pl.when(both)
        def _():
            arrive(1, p)
            attend(1, second, p)

    load_weight.wait()
    width = weight.shape[1] // chunks

    def rows(p, who):
        return jnp.concatenate(
            [
                att[p, pl.ds(pl.multiple_of((r * 2 + who) * slab, slab), slab), :]
                for r in (row, 1 - row)
            ],
            axis=0,
        )

    def give_a(p, c):
        return pltpu.make_async_remote_copy(
            src_ref=send_a.at[p, c], dst_ref=recv_a.at[p, c],
            send_sem=a_send.at[p, c], recv_sem=a_recv.at[p, c],
            device_id={"sub": 1 - core}, device_id_type=MESH,
        )

    def give_b(p, c):
        return pltpu.make_async_remote_copy(
            src_ref=send_b.at[p, c], dst_ref=recv_b.at[p, c],
            send_sem=b_send.at[p, c], recv_sem=b_recv.at[p, c],
            device_id={"head": 1 - row}, device_id_type=MESH,
        )

    for p in range(pieces):
        for h in range(heads):

            @pl.when(frame != owner[h])
            def _():
                here = att.at[p, :, h * HEAD : (h + 1) * HEAD]
                pltpu.make_async_copy(here, here, back_recv.at[p, h]).wait()

        tokens = jnp.concatenate([rows(p, 1 - core), rows(p, core)], axis=0)
        for c in range(chunks):
            share = jnp.dot(
                tokens, weight[:, c * width : (c + 1) * width], preferred_element_type=jnp.float32
            )
            send_a[p, c] = share[: 2 * slab].astype(jnp.bfloat16)
            give_a(p, c).start()
            own[c] = share[2 * slab :]
        for c in range(chunks):
            give_a(p, c).wait_recv()
            both_cores = own[c] + recv_a[p, c].astype(jnp.float32)
            send_b[p, c] = both_cores[slab:].astype(jnp.bfloat16)
            give_b(p, c).start()
            acc[p, c] = both_cores[:slab]

    for p in range(pieces):
        for c in range(chunks):
            give_b(p, c).wait_recv()
            out_ref[p * slab : (p + 1) * slab, c * width : (c + 1) * width] = (
                acc[p, c] + recv_b[p, c].astype(jnp.float32)
            ).astype(jnp.bfloat16)

    for p in range(pieces):
        for c in range(chunks):
            give_a(p, c).wait_send()
            give_b(p, c).wait_send()
    for h in range(heads):

        @pl.when(frame != owner[h])
        def _():
            for a in range(2 + pieces):
                outgoing(h, a).wait_send()

    for i in range(n):

        @pl.when(i != frame)
        def _():
            for p in range(pieces):
                returning(0, first, p, i).wait_send()

        @pl.when(jnp.logical_and(both, i != frame))
        def _():
            for p in range(pieces):
                returning(1, second, p, i).wait_send()


def fused(n, queries, keys, values, band_table, windows, out_weight):
    length, width = queries.shape[1:]
    columns = out_weight.shape[1]
    heads = width // HEAD
    block = length // 4
    chunks = 2
    pieces = 2
    slab = block // pieces
    part = columns // chunks
    anywhere = pl.BlockSpec(memory_space=pl.ANY)
    dma = pltpu.SemaphoreType.DMA
    mixed = pl.pallas_call(
        functools.partial(fused_kernel, n, pieces, chunks),
        out_shape=jax.ShapeDtypeStruct((block, columns), jnp.bfloat16),
        in_specs=[anywhere] * 6,
        out_specs=pl.BlockSpec(memory_space=pltpu.VMEM),
        scratch_shapes=[
            pltpu.SMEM(band_table.shape, jnp.int32),
            pltpu.SMEM(windows.shape, jnp.int32),
            pltpu.VMEM((2, pieces, n, 4, slab, HEAD), jnp.bfloat16),
            pltpu.VMEM((2, 2, n, length, HEAD), jnp.bfloat16),
            pltpu.VMEM(out_weight.shape, jnp.bfloat16),
            pltpu.VMEM((2, pieces, n, 4 * slab, HEAD), jnp.bfloat16),
            pltpu.VMEM((pieces, 4 * slab, width), jnp.bfloat16),
            pltpu.VMEM((pieces, chunks, 2 * slab, part), jnp.bfloat16),
            pltpu.VMEM((pieces, chunks, 2 * slab, part), jnp.bfloat16),
            pltpu.VMEM((pieces, chunks, slab, part), jnp.bfloat16),
            pltpu.VMEM((pieces, chunks, slab, part), jnp.bfloat16),
            pltpu.VMEM((pieces, chunks, slab, part), jnp.float32),
            pltpu.VMEM((chunks, 2 * slab, part), jnp.float32),
            dma((heads, 2 + pieces)),
            dma((2, 2 + pieces, n)),
            dma((2, pieces, n)),
            dma((pieces, heads)),
            dma((pieces, chunks)),
            dma((pieces, chunks)),
            dma((pieces, chunks)),
            dma((pieces, chunks)),
            dma,
            dma((2,)),
        ],
        compiler_params=pltpu.CompilerParams(
            collective_id=0, has_side_effects=True, vmem_limit_bytes=60 * 1024 * 1024
        ),
    )(queries.reshape(4, block, width), keys, values, band_table, windows, out_weight)
    return mixed[None]


def solution(mesh):
    n = mesh.shape["tm"]

    def step(queries, keys, values, band_table, windows, out_weight):
        paired = mesh.shape["head"] == 2 and mesh.shape["sub"] == 2
        if n > 2 and paired and queries.shape[0] == 1 and queries.shape[2] == (2 * n - 2) * HEAD:
            return fused(n, queries, keys, values, band_table, windows, out_weight)
        return local(queries, keys, values, band_table, windows, out_weight)

    return jax.shard_map(
        step,
        mesh=mesh,
        in_specs=(
            P(("clip", "tm"), None, ("head", "sub")),
            P(("clip", "tm"), None, ("head", "sub")),
            P(("clip", "tm"), None, ("head", "sub")),
            P(),
            P(),
            P(("head", "sub"), None),
        ),
        out_specs=P(("clip", "tm"), ("head", "sub"), None),
        check_vma=False,
    )
```

```python
import functools

import jax
import jax.numpy as jnp
from jax import lax
from jax.experimental import pallas as pl
from jax.experimental.pallas import tpu as pltpu
from jax.sharding import PartitionSpec as P

HEAD = 128
MESH = pl.DeviceIdType.MESH


def local(queries, keys, values, band_table, windows, out_weight):
    frames, length, width = queries.shape
    heads = width // HEAD
    scale = HEAD ** (-0.5)
    here = lax.axis_index("tm") * frames
    query = queries[0].reshape(length, heads, HEAD)
    places = lax.iota(jnp.int32, length)
    gap = jnp.abs(places[:, None] - places[None, :])

    def absorb(carry, key_frame, value_frame, frame, usable):
        peak, total, numer = carry
        reach = windows[band_table[here, frame]]
        allowed = (gap <= reach)[None] & usable
        scores = (
            jnp.einsum(
                "phd,qhd->hpq",
                query,
                key_frame.reshape(length, heads, HEAD),
                preferred_element_type=jnp.float32,
            )
            * scale
        )
        masked = jnp.where(allowed, scores, jnp.float32(-1e30))
        top = jnp.maximum(peak, jnp.max(masked, axis=-1))
        weights = jnp.where(allowed, jnp.exp(scores - top[:, :, None]), jnp.float32(0.0))
        shrink = jnp.exp(peak - top)
        total = total * shrink + jnp.sum(weights, axis=-1)
        added = jnp.einsum(
            "hpq,qhd->phd",
            weights.astype(jnp.bfloat16),
            value_frame.reshape(length, heads, HEAD),
            preferred_element_type=jnp.float32,
        )
        numer = numer * jnp.transpose(shrink)[:, :, None] + added
        return (top, total, numer)

    carry = (
        jnp.full((heads, length), -1e30, jnp.float32),
        jnp.zeros((heads, length), jnp.float32),
        jnp.zeros((length, heads, HEAD), jnp.float32),
    )
    skipped = -1
    state = carry
    key_part = lax.all_gather(keys, "tm", axis=0, tiled=True)
    value_part = lax.all_gather(values, "tm", axis=0, tiled=True)

    def advance(inner, item):
        key_frame, value_frame, offset = item
        usable = jnp.abs(offset - here) > skipped
        return (absorb(inner, key_frame, value_frame, offset, usable), None)

    state, unused = lax.scan(
        advance, state, (key_part, value_part, lax.iota(jnp.int32, key_part.shape[0]))
    )
    carry = state
    peak, total, numer = carry
    attended = (
        (numer / jnp.transpose(total)[:, :, None]).astype(jnp.bfloat16).reshape(length, width)
    )
    mixed = lax.psum_scatter(
        jnp.dot(attended, out_weight, preferred_element_type=jnp.float32).astype(jnp.bfloat16),
        ("head", "sub"),
        scatter_dimension=0,
        tiled=True,
    )
    return mixed[None]


def fused_kernel(
    n, pieces, chunks, q_hbm, k_hbm, v_hbm, band_hbm, windows_hbm, w_hbm, out_ref,
    band, windows, asked, buf, weight, done, att, send_a, recv_a, send_b, recv_b, acc, own,
    in_send, in_recv, back_send, back_recv, a_send, a_recv, b_send, b_recv, w_sem, table_sem,
):
    frame = lax.axis_index("tm")
    row = lax.axis_index("head")
    core = lax.axis_index("sub")
    length = k_hbm.shape[1]
    block = length // 4
    slab = block // pieces
    heads = 2 * n - 2
    owner = [(h + 1) // 2 for h in range(heads)]
    slot = [1 if h > 0 and h % 2 == 0 else 0 for h in range(heads)]
    scale = HEAD ** (-0.5)

    barrier = pltpu.get_barrier_semaphore()
    for step in range(1, n):
        pl.semaphore_signal(
            barrier, inc=1, device_id={"tm": lax.rem(frame + step, n)}, device_id_type=MESH
        )
    pl.semaphore_signal(barrier, inc=1, device_id={"head": 1 - row}, device_id_type=MESH)
    pl.semaphore_signal(barrier, inc=1, device_id={"sub": 1 - core}, device_id_type=MESH)
    pl.semaphore_wait(barrier, n + 1)

    low = frame < n // 2

    def ends(h, a):
        columns = slice(h * HEAD, (h + 1) * HEAD)
        if a < 2:
            return (k_hbm, v_hbm)[a].at[0, :, columns], buf.at[slot[h], a, frame]
        p = a - 2
        source = q_hbm.at[:, p * slab : (p + 1) * slab, columns]
        return source, asked.at[slot[h], p, frame]

    def outgoing(h, a):
        source, target = ends(h, a)
        return pltpu.make_async_remote_copy(
            src_ref=source,
            dst_ref=target,
            send_sem=in_send.at[h, a],
            recv_sem=in_recv.at[slot[h], a, frame],
            device_id={"tm": owner[h]},
            device_id_type=MESH,
        )

    def send_head(h, ready, which):
        @pl.when(jnp.logical_and(ready, frame != owner[h]))
        def _():
            for a in which:
                outgoing(h, a).start()

    def send_slot(s, which):
        below = [h for h in range(heads) if slot[h] == s and owner[h] < n // 2]
        above = [h for h in reversed(range(heads)) if slot[h] == s and owner[h] >= n // 2]
        for h in above:
            send_head(h, low, which)
        for h in below:
            send_head(h, frame >= 0, which)
        for h in above:
            send_head(h, jnp.logical_not(low), which)

    send_slot(1, (0, 2))
    send_slot(0, (0, 2))
    send_slot(1, (1,))
    send_slot(0, (1,))
    for p in range(1, pieces):
        send_slot(1, (2 + p,))
        send_slot(0, (2 + p,))
    for h in range(heads):

        @pl.when(frame == owner[h])
        def _():
            for a in range(2 + pieces):
                source, target = ends(h, a)
                pltpu.make_async_copy(source, target, in_recv.at[slot[h], a, frame]).start()

    load_weight = pltpu.make_async_copy(w_hbm, weight, w_sem)
    load_weight.start()
    tables = (
        pltpu.make_async_copy(band_hbm, band, table_sem.at[0]),
        pltpu.make_async_copy(windows_hbm, windows, table_sem.at[1]),
    )
    for table in tables:
        table.start()

    for table in tables:
        table.wait()
    height = 4 * slab
    spot = lax.broadcasted_iota(jnp.int32, (height, length), 0)
    spot = (spot // slab) * block + lax.rem(spot, slab)
    spot = spot - lax.broadcasted_iota(jnp.int32, (height, length), 1)

    def returning(s, h, p, i):
        return pltpu.make_async_remote_copy(
            src_ref=done.at[s, p, i],
            dst_ref=att.at[p, :, pl.ds(pl.multiple_of(h * HEAD, HEAD), HEAD)],
            send_sem=back_send.at[s, p, i],
            recv_sem=back_recv.at[p, h],
            device_id={"tm": i},
            device_id_type=MESH,
        )

    def arrive(s, p):
        for j in range(n):
            for a in (0, 1) if p == 0 else ():
                pltpu.make_async_copy(buf.at[s, a, j], buf.at[s, a, j], in_recv.at[s, a, j]).wait()
            here = asked.at[s, p, j]
            pltpu.make_async_copy(here, here, in_recv.at[s, 2 + p, j]).wait()

    def attend(s, h, p):
        gap = jnp.abs(spot + p * slab)

        def one(step, carry):
            i = lax.rem(frame + 1 + step, n)
            query = asked[s, p, i].reshape(height, HEAD)
            parts = []
            top = None
            for j in range(n):
                score = lax.dot_general(
                    query, buf[s, 0, j], (((1,), (1,)), ((), ())),
                    preferred_element_type=jnp.float32,
                ) * scale
                score = jnp.where(gap <= windows[band[i, j]], score, jnp.float32(-1e30))
                peak = jnp.max(score, axis=-1, keepdims=True)
                top = peak if top is None else jnp.maximum(top, peak)
                parts.append(score)
            total = None
            numer = None
            for j in range(n):
                part = jnp.exp(parts[j] - top)
                added = jnp.sum(part, axis=-1, keepdims=True)
                product = jnp.dot(
                    part.astype(jnp.bfloat16), buf[s, 1, j], preferred_element_type=jnp.float32
                )
                total = added if total is None else total + added
                numer = product if numer is None else numer + product
            result = (numer / total).astype(jnp.bfloat16)

            @pl.when(i != frame)
            def _():
                done[s, p, i] = result
                returning(s, h, p, i).start()

            @pl.when(i == frame)
            def _():
                att[p, :, pl.ds(pl.multiple_of(h * HEAD, HEAD), HEAD)] = result

            return carry

        lax.fori_loop(0, n, one, 0)

    first = 2 * frame - (frame + n - 1) // n
    second = 2 * frame
    both = jnp.logical_and(frame > 0, frame < n - 1)
    for p in range(pieces):
        @pl.when(both)
        def _():
            arrive(1, p)
            attend(1, second, p)

        arrive(0, p)
        attend(0, first, p)

    load_weight.wait()
    width = weight.shape[1] // chunks

    def rows(p, who):
        return jnp.concatenate(
            [
                att[p, pl.ds(pl.multiple_of((r * 2 + who) * slab, slab), slab), :]
                for r in (row, 1 - row)
            ],
            axis=0,
        )

    def give_a(p, c):
        return pltpu.make_async_remote_copy(
            src_ref=send_a.at[p, c], dst_ref=recv_a.at[p, c],
            send_sem=a_send.at[p, c], recv_sem=a_recv.at[p, c],
            device_id={"sub": 1 - core}, device_id_type=MESH,
        )

    def give_b(p, c):
        return pltpu.make_async_remote_copy(
            src_ref=send_b.at[p, c], dst_ref=recv_b.at[p, c],
            send_sem=b_send.at[p, c], recv_sem=b_recv.at[p, c],
            device_id={"head": 1 - row}, device_id_type=MESH,
        )

    for p in range(pieces):
        for h in range(heads):

            @pl.when(frame != owner[h])
            def _():
                here = att.at[p, :, h * HEAD : (h + 1) * HEAD]
                pltpu.make_async_copy(here, here, back_recv.at[p, h]).wait()

        tokens = jnp.concatenate([rows(p, 1 - core), rows(p, core)], axis=0)
        for c in range(chunks):
            share = jnp.dot(
                tokens, weight[:, c * width : (c + 1) * width], preferred_element_type=jnp.float32
            )
            send_a[p, c] = share[: 2 * slab].astype(jnp.bfloat16)
            give_a(p, c).start()
            own[c] = share[2 * slab :]
        for c in range(chunks):
            give_a(p, c).wait_recv()
            both_cores = own[c] + recv_a[p, c].astype(jnp.float32)
            send_b[p, c] = both_cores[slab:].astype(jnp.bfloat16)
            give_b(p, c).start()
            acc[p, c] = both_cores[:slab]

    for p in range(pieces):
        for c in range(chunks):
            give_b(p, c).wait_recv()
            out_ref[p * slab : (p + 1) * slab, c * width : (c + 1) * width] = (
                acc[p, c] + recv_b[p, c].astype(jnp.float32)
            ).astype(jnp.bfloat16)

    for p in range(pieces):
        for c in range(chunks):
            give_a(p, c).wait_send()
            give_b(p, c).wait_send()
    for h in range(heads):

        @pl.when(frame != owner[h])
        def _():
            for a in range(2 + pieces):
                outgoing(h, a).wait_send()

    for i in range(n):

        @pl.when(i != frame)
        def _():
            for p in range(pieces):
                returning(0, first, p, i).wait_send()

        @pl.when(jnp.logical_and(both, i != frame))
        def _():
            for p in range(pieces):
                returning(1, second, p, i).wait_send()


def fused(n, queries, keys, values, band_table, windows, out_weight):
    length, width = queries.shape[1:]
    columns = out_weight.shape[1]
    heads = width // HEAD
    block = length // 4
    chunks = 2
    pieces = 2
    slab = block // pieces
    part = columns // chunks
    anywhere = pl.BlockSpec(memory_space=pl.ANY)
    dma = pltpu.SemaphoreType.DMA
    mixed = pl.pallas_call(
        functools.partial(fused_kernel, n, pieces, chunks),
        out_shape=jax.ShapeDtypeStruct((block, columns), jnp.bfloat16),
        in_specs=[anywhere] * 6,
        out_specs=pl.BlockSpec(memory_space=pltpu.VMEM),
        scratch_shapes=[
            pltpu.SMEM(band_table.shape, jnp.int32),
            pltpu.SMEM(windows.shape, jnp.int32),
            pltpu.VMEM((2, pieces, n, 4, slab, HEAD), jnp.bfloat16),
            pltpu.VMEM((2, 2, n, length, HEAD), jnp.bfloat16),
            pltpu.VMEM(out_weight.shape, jnp.bfloat16),
            pltpu.VMEM((2, pieces, n, 4 * slab, HEAD), jnp.bfloat16),
            pltpu.VMEM((pieces, 4 * slab, width), jnp.bfloat16),
            pltpu.VMEM((pieces, chunks, 2 * slab, part), jnp.bfloat16),
            pltpu.VMEM((pieces, chunks, 2 * slab, part), jnp.bfloat16),
            pltpu.VMEM((pieces, chunks, slab, part), jnp.bfloat16),
            pltpu.VMEM((pieces, chunks, slab, part), jnp.bfloat16),
            pltpu.VMEM((pieces, chunks, slab, part), jnp.float32),
            pltpu.VMEM((chunks, 2 * slab, part), jnp.float32),
            dma((heads, 2 + pieces)),
            dma((2, 2 + pieces, n)),
            dma((2, pieces, n)),
            dma((pieces, heads)),
            dma((pieces, chunks)),
            dma((pieces, chunks)),
            dma((pieces, chunks)),
            dma((pieces, chunks)),
            dma,
            dma((2,)),
        ],
        compiler_params=pltpu.CompilerParams(
            collective_id=0, has_side_effects=True, vmem_limit_bytes=60 * 1024 * 1024
        ),
    )(queries.reshape(4, block, width), keys, values, band_table, windows, out_weight)
    return mixed[None]


def solution(mesh):
    n = mesh.shape["tm"]

    def step(queries, keys, values, band_table, windows, out_weight):
        paired = mesh.shape["head"] == 2 and mesh.shape["sub"] == 2
        if n > 2 and paired and queries.shape[0] == 1 and queries.shape[2] == (2 * n - 2) * HEAD:
            return fused(n, queries, keys, values, band_table, windows, out_weight)
        return local(queries, keys, values, band_table, windows, out_weight)

    return jax.shard_map(
        step,
        mesh=mesh,
        in_specs=(
            P(("clip", "tm"), None, ("head", "sub")),
            P(("clip", "tm"), None, ("head", "sub")),
            P(("clip", "tm"), None, ("head", "sub")),
            P(),
            P(),
            P(("head", "sub"), None),
        ),
        out_specs=P(("clip", "tm"), ("head", "sub"), None),
        check_vma=False,
    )
```
